32 devices in a mesh: group: 8 (over y, x, core), tp: 4 (over z).
Axes of the slice: x: 2, y: 2, z: 4, core: 2. Of those that a mesh axis runs over, the one named last changes fastest.
Arguments:
- hidden: bfloat16 [2048, 8192], P('group', 'tp'), may hold values from -6 to 6
- w_kv: bfloat16 [8192, 2048], P('tp'), may hold values from -0.0625 to 0.0625
- prompt_lengths: int32 [2, 8], replicated, may hold values from 1 to 128, 256 in all within a row
- owner_step: int32 [2, 8], replicated, may hold values from 1 to 3
- cache: bfloat16 [64, 128, 2048], P(('group', 'tp')), may hold values from -8 to 8
- cache_len: int32 [64], P(('group', 'tp')), may hold values from 1 to 128
- queries: bfloat16 [64, 8192], P('group', 'tp'), may hold values from -200 to 200
- fresh: bfloat16 [64, 2048], P('group', 'tp'), may hold values from -10 to 10
- logits: bfloat16 [64, 30720], P('group', 'tp'), may hold values from -300 to 300
- states: int32 [64], P('group'), may hold values from 0 to 23
- masks: int32 [24, 1024], P(None, 'tp'), may hold values from 0 to 1073741823, as said below
Outputs:
- attended: bfloat16 [64, 8192], P('group', 'tp')
- logprob: float32 [64, 30720], P('group', 'tp')
The draws below stay inside these ranges and needn't reach their ends.
Inputs may be any that keep to these rules, and one draw needn't show every extreme that they name: `prompt_lengths`: each row sums to 256; the longest prompt of every row has exactly 128 tokens. Prompt k of prefill group p goes to group p + owner_step[p, k] * 2. `masks`: every state allows at least one token in each aligned block of 7680 vocabulary entries.
All inputs are finite; a program needn't handle non-finite values.
Results may differ from the reference program's by a relative error of at most 0.02.
Values may be sent and summed in bfloat16 or wider, within the bound.
A program may use at most 64 MiB of HBM per device.

```python
import math
import jax
import jax.numpy as jnp
import numpy as np
from jax import lax

D = 8192
HEADS = 64
KVH = 8
HD = 128
VOC_DEV = 7680
BLOCK = 256
MAXLEN = 128
CACHE = 128
STATES = 24
REQ_DEV = 2
REQUESTS = 8
PROMPTS = 8
VOCAB = 30720
PREFILL = 2
N_GROUP = 8
N_TP = 4


def anchor_draw(key):
    base = jax.random.fold_in(key, 901)
    chosen_rows = jax.random.permutation(jax.random.fold_in(base, 1), PREFILL * REQUESTS)[:6]
    anchors = jnp.clip(jax.random.normal(jax.random.fold_in(base, 2), (6, KVH * HD), jnp.float32), -4.0, 4.0)
    return (chosen_rows, anchors)


def draw_cache(key, part):
    shape = (N_GROUP * REQUESTS, CACHE, 2 * KVH * HD)
    values = jnp.clip(jax.random.normal(jax.random.fold_in(key, 11), shape, jnp.float32), -6.0, 6.0)
    chosen_rows, anchors = anchor_draw(key)
    values = values.at[chosen_rows, 0, :KVH * HD].set(anchors)
    return values.astype(jnp.bfloat16)


def draw_queries(key, part):
    shape = (N_GROUP * REQUESTS, HEADS * HD)
    values = jnp.clip(jax.random.normal(jax.random.fold_in(key, 21), shape, jnp.float32), -6.0, 6.0)
    return values.astype(jnp.bfloat16)


def draw_fresh(key, part):
    shape = (N_GROUP * REQUESTS, 2 * KVH * HD)
    values = jnp.clip(jax.random.normal(jax.random.fold_in(key, 31), shape, jnp.float32), -6.0, 6.0)
    return values.astype(jnp.bfloat16)


def draw_logits(key, part):
    shape = (N_GROUP * REQUESTS, VOCAB)
    ramp = 1.5 * jnp.arange(VOCAB, dtype=jnp.float32) / VOCAB
    values = 3.0 * jnp.clip(jax.random.normal(jax.random.fold_in(key, 41), shape, jnp.float32), -8.0, 8.0) + ramp[None, :]
    return values.astype(jnp.bfloat16)


def draw_masks(key, part):
    word_count = VOCAB // 30
    packed = jax.random.randint(jax.random.fold_in(key, 51), (STATES, word_count), 0, 1073741824, jnp.int32)
    forced = jnp.left_shift(jnp.ones((STATES, word_count), jnp.int32), jax.random.randint(jax.random.fold_in(key, 52), (STATES, word_count), 0, 30, jnp.int32))
    leading = jnp.arange(word_count, dtype=jnp.int32) % (VOC_DEV // 30) == 0
    return jnp.where(leading[None, :], jnp.bitwise_or(packed, forced), packed).astype(jnp.int32)


def touch_ends(values, rng, low, largest):
    extent = values.shape
    spot = [jax.random.randint(jax.random.fold_in(rng, axis), (), 0, extent[axis]) for axis in range(len(extent))]
    values = values.at[tuple(spot)].set(low)
    longest = extent.index(max(extent))
    spot[longest] = (spot[longest] + 1) % extent[longest]
    return values.at[tuple(spot)].set(largest)


def shard_levels(rng, shape, cuts, low, high):
    def one(dim, blocks):
        steps = jax.random.uniform(jax.random.fold_in(jax.random.fold_in(rng, 6), dim), (blocks,), jnp.float32, low / len(cuts), high / len(cuts))
        return jnp.repeat(jnp.exp(steps), shape[dim] // blocks).reshape((-1,) + (1,) * (len(shape) - dim - 1))

    factor_of = one(*cuts[0])
    for cut in cuts[1:]:
        factor_of = factor_of * one(*cut)
    return factor_of


def profile(count, total, limit, slope):
    weights = [(1 << 20) // math.isqrt(rank ** slope) + 1 for rank in range(2, count + 1)]
    surplus, holding = total - limit - (count - 1), [1] * (count - 1)
    while surplus > 0:
        movable = [i for i in range(count - 1) if holding[i] < limit]
        whole, remaining = sum([weights[i] for i in movable]), surplus
        for i in movable:
            extra = min(limit - holding[i], max(1, remaining * weights[i] // whole), surplus)
            holding[i] = holding[i] + extra
            surplus = surplus - extra
    return np.array([limit] + holding)


def uneven_parts(key, count, total, limit, slope):
    if count == 2:
        one = jax.random.randint(key, (), max(1, total - limit), min(limit, total - 1) + 1)
        return jnp.stack([one, total - one])
    tallies = jnp.asarray(profile(count, total, limit, slope), jnp.int32)
    twos = (count - 1) // 2
    giver, sink = tallies[1:1 + 2 * twos:2], tallies[2:2 + 2 * twos:2]
    slack = jnp.minimum(giver - 1, limit - sink)
    moved = jax.random.randint(jax.random.fold_in(key, 1), (twos,), 0, 1 << 20) % (slack + 1)
    tallies = tallies.at[1:1 + 2 * twos:2].set(giver - moved).at[2:2 + 2 * twos:2].set(sink + moved)
    return tallies[jax.random.permutation(jax.random.fold_in(key, 2), count)]


def normal_values(key, dims, scale, bound, pieces=(), kind=jnp.bfloat16):
    entries = jax.random.normal(key, dims, jnp.float32) * scale
    if len(pieces) > 0:
        entries = shard_levels(key, dims, pieces, -0.22, 0.18) * entries
    return jnp.clip(entries, min=-bound, max=bound).astype(kind)


def setup_inputs(seed: int = 0) -> dict:
    key_list = jax.random.split(jax.random.key(seed), 12)
    return {
        "hidden": normal_values(key_list[0], (N_GROUP * BLOCK, D), 1.0, 6.0, ((0, 8), (1, 4))),
        "w_kv": normal_values(key_list[1], (D, 2 * KVH * HD), D ** -0.5, 0.0625, ((0, 4),)),
        "prompt_lengths": jax.vmap(lambda own: uneven_parts(own, PROMPTS, BLOCK, MAXLEN, 2))(jax.random.split(key_list[2], PREFILL)).reshape((PREFILL, PROMPTS)).astype(jnp.int32),
        "owner_step": touch_ends(jax.random.randint(key_list[3], (PREFILL, PROMPTS), 1, 4), jax.random.fold_in(key_list[3], 1), 1, 3).astype(jnp.int32),
        "cache": draw_cache(jax.random.fold_in(key_list[11], 71), 0),
        "cache_len": touch_ends(jax.random.randint(key_list[5], (N_GROUP * REQUESTS,), 1, CACHE + 1), jax.random.fold_in(key_list[5], 1), 1, CACHE).astype(jnp.int32),
        "queries": draw_queries(jax.random.fold_in(key_list[11], 71), 0),
        "fresh": draw_fresh(jax.random.fold_in(key_list[11], 71), 0),
        "logits": draw_logits(jax.random.fold_in(key_list[11], 71), 0),
        "states": touch_ends(jax.random.randint(key_list[9], (N_GROUP * REQUESTS,), 0, STATES), jax.random.fold_in(key_list[9], 1), 0, STATES - 1).astype(jnp.int32),
        "masks": draw_masks(jax.random.fold_in(key_list[11], 71), 0),
    }


def landing(slot_ids, source, turn_index, prompt_lengths, owner_step):
    chosen = owner_step[source] == turn_index
    ranking = jnp.cumsum(chosen.astype(jnp.int32)) - 1
    arrivals = jnp.sum(chosen.astype(jnp.int32))
    matched = chosen[None, :] & (ranking[None, :] == slot_ids[:, None])
    lengths = prompt_lengths[source]
    starts = jnp.cumsum(lengths) - lengths
    first_row = lax.optimization_barrier(jnp.sum(jnp.where(matched, starts[None, :], 0), axis=1)).astype(jnp.int32)
    prompt_len = lax.optimization_barrier(jnp.sum(jnp.where(matched, lengths[None, :], 0), axis=1)).astype(jnp.int32)
    landed = (slot_ids < arrivals) & (turn_index >= 1)
    return (landed, first_row, prompt_len)

def attend(query_rows, merged, alive_len, fresh_rows):
    row_count = merged.shape[0]
    group_size = HEADS // KVH
    key_rows = merged[:, :, :KVH * HD].astype(jnp.float32).reshape(row_count, CACHE, KVH, HD)
    value_rows = merged[:, :, KVH * HD:].astype(jnp.float32).reshape(row_count, CACHE, KVH, HD)
    queries = query_rows.astype(jnp.float32).reshape(row_count, KVH, group_size, HD)
    own_key = fresh_rows[:, :KVH * HD].astype(jnp.float32).reshape(row_count, KVH, HD)
    own_value = fresh_rows[:, KVH * HD:].astype(jnp.float32).reshape(row_count, KVH, HD)
    scaling = 1.0 / math.sqrt(HD)
    scores = jnp.einsum('rkgd,rtkd->rkgt', queries, key_rows) * scaling
    own_score = jnp.einsum('rkgd,rkd->rkg', queries, own_key) * scaling
    positions = jnp.arange(CACHE, dtype=jnp.int32)
    alive_mask = (positions[None, :] < alive_len[:, None])[:, None, None, :]
    highest = jnp.maximum(lax.optimization_barrier(jnp.max(jnp.where(alive_mask, scores, -jnp.inf), axis=3)), own_score)
    exponent = jnp.where(alive_mask, jnp.exp(scores - highest[..., None]), 0.0)
    own_exponent = jnp.exp(own_score - highest)
    denominator = lax.optimization_barrier(jnp.sum(exponent, axis=3)) + own_exponent
    weights = lax.optimization_barrier((exponent / denominator[..., None]).astype(jnp.bfloat16)).astype(jnp.float32)
    own_weight = lax.optimization_barrier((own_exponent / denominator).astype(jnp.bfloat16)).astype(jnp.float32)
    attended = jnp.einsum('rkgt,rtkd->rkgd', weights, value_rows)
    attended = attended + own_weight[..., None] * own_value[:, :, None, :]
    return attended.reshape(row_count, HEADS * HD).astype(jnp.bfloat16)

def reference(hidden, w_kv, prompt_lengths, owner_step, cache, cache_len, queries, fresh, logits, states, masks):
    blocks = hidden.reshape(N_GROUP, BLOCK, D)[:PREFILL]
    projected = lax.map(lambda hidden_block: jnp.dot(hidden_block, w_kv, preferred_element_type=jnp.float32).astype(jnp.bfloat16), blocks)
    padded = jnp.pad(projected, ((0, 0), (0, MAXLEN), (0, 0)))
    local_ids = jnp.arange(REQUESTS, dtype=jnp.int32)
    slot_ids = local_ids % REQ_DEV * N_TP + local_ids // REQ_DEV

    def decode_group(items):
        group_index, cache_rows, alive_len, query_rows, fresh_rows = items
        source = group_index % PREFILL
        turn_index = group_index // PREFILL
        landed, first_row, prompt_len = landing(slot_ids, source, turn_index, prompt_lengths, owner_step)
        source_rows = padded[source]
        handed = jax.vmap(lambda offset: lax.dynamic_slice_in_dim(source_rows, offset, MAXLEN, 0))(first_row)
        front = jnp.where(landed[:, None, None], handed, cache_rows[:, :MAXLEN])
        merged = jnp.concatenate([front, cache_rows[:, MAXLEN:]], axis=1)
        alive = jnp.where(landed, prompt_len, alive_len)
        return attend(query_rows, merged, alive, fresh_rows)
    attended = lax.map(decode_group, (jnp.arange(N_GROUP, dtype=jnp.int32), cache.reshape(N_GROUP, REQUESTS, CACHE, 2 * KVH * HD), cache_len.reshape(N_GROUP, REQUESTS), queries.reshape(N_GROUP, REQUESTS, HEADS * HD), fresh.reshape(N_GROUP, REQUESTS, 2 * KVH * HD)))
    attended = attended.reshape(N_GROUP * REQUESTS, HEADS * HD)

    def grammar_rows(items):
        logit_rows, state_ids = items
        packed = masks[state_ids]
        shifts = jnp.arange(30, dtype=jnp.int32)
        bit_flags = jnp.bitwise_and(jnp.right_shift(packed[:, :, None], shifts[None, None, :]), 1)
        permitted = bit_flags.reshape(packed.shape[0], VOCAB) == 1
        values = logit_rows.astype(jnp.float32)
        highest = lax.optimization_barrier(jnp.max(jnp.where(permitted, values, -jnp.inf), axis=1))
        denominator = lax.optimization_barrier(jnp.sum(jnp.where(permitted, jnp.exp(values - highest[:, None]), 0.0), axis=1))
        normalizer = highest + jnp.log(denominator)
        return jnp.where(permitted, values - normalizer[:, None], 0.0)
    logprob = lax.map(grammar_rows, (logits.reshape(N_GROUP, REQUESTS, VOCAB), states.reshape(N_GROUP, REQUESTS)))
    return (attended, logprob.reshape(N_GROUP * REQUESTS, VOCAB))
```

```python
import functools
import math

import jax
import jax.numpy as jnp
from jax import lax
from jax.experimental import pallas as pl
from jax.experimental.pallas import tpu as pltpu
from jax.sharding import PartitionSpec as P

HEADS = 64
KVH = 8
HD = 128
GQ = HEADS // KVH
TURNS = 4
BITS = 30
MESH = pl.DeviceIdType.MESH
F32 = jnp.float32
BF16 = jnp.bfloat16


def segments(block):
    u = block // 8
    return (
        (0, 0, 2 * u, 0),
        (0, 2 * u, 2 * u, 2 * u),
        (1, 4 * u, u, 0),
        (2, 5 * u, 2 * u, 0),
        (3, 7 * u, u, 0),
    )


def kernel(
    n, groups,
    plen, ostep, clen, states, hidden, w_kv, cache, queries, fresh, logits, masks,
    att_out, lp_out,
    hid, w, part, rsbuf, kv, cv, qv, frv, lgv, mkv, packed, qs, qrecv, osend, orecv,
    frall, stat, lp, att,
    lsem, wsem, hsend, hrecv, rssend, rsrecv, agsend, agrecv,
    qsend, qrsem, fsend, frsem, osem, orsem, ssend, srsem,
):
    g = lax.axis_index("group")
    c = lax.axis_index("tp")
    prefill = groups // TURNS
    p = lax.rem(g, prefill)
    turn = g // prefill
    block, dl = hidden.shape
    rows, vdev = logits.shape
    own = cache.shape[0]
    npos = cache.shape[1]
    hq = HEADS // n
    gq = min(GQ, hq)
    kh = max(1, hq // GQ)
    kw = kh * HD
    oh = own * hq
    fw = fresh.shape[1]
    half = KVH * HD
    segs = segments(block)
    scale = 1.0 / math.sqrt(HD)

    def peer(o):
        return lax.rem(c + o, n)

    def kv_first(d):
        return (d * hq) // GQ

    barrier = pltpu.get_barrier_semaphore()

    def hello(o, carry):
        pl.semaphore_signal(barrier, inc=1, device_id=(g, peer(o)), device_id_type=MESH)
        return carry

    lax.fori_loop(1, n, hello, 0)
    for o in range(1, TURNS):
        pl.semaphore_signal(
            barrier, inc=1, device_id=(lax.rem(g + o * prefill, groups), c), device_id_type=MESH
        )

    small = [
        pltpu.make_async_copy(src, dst, lsem.at[i])
        for i, (src, dst) in enumerate(
            ((queries, qv), (fresh, frv), (logits, lgv), (cache, cv))
        )
    ]
    small += [
        pltpu.make_async_copy(masks.at[:, k * HD : (k + 1) * HD], mkv.at[k], lsem.at[6 + k])
        for k in range(mkv.shape[0])
    ]
    own_tokens = part.shape[1]
    own_hidden = pltpu.make_async_copy(hidden.at[pl.ds(0, own_tokens)], hid, lsem.at[5])

    def w_copies(d):
        first = pl.multiple_of(kv_first(d) * HD, HD)
        return [
            pltpu.make_async_copy(
                w_kv.at[:, pl.ds(pl.multiple_of(first + s * half, HD), kw)],
                w.at[d, :, pl.ds(s * kw, kw)],
                wsem.at[d, s],
            )
            for s in range(2)
        ]

    small[0].start()
    small[1].start()

    @pl.when(turn == 0)
    def _():
        own_hidden.start()

    def start_w(o, carry):
        for copy in w_copies(peer(o)):
            copy.start()
        return carry

    lax.fori_loop(1, n, start_w, 0)
    for copy in small[2:]:
        copy.start()
    start_w(0, 0)

    pl.semaphore_wait(barrier, n - 1 + TURNS - 1)

    def spread(t, start, size, loff):
        return pltpu.make_async_remote_copy(
            src_ref=hidden.at[pl.ds(start, size)],
            dst_ref=hid.at[pl.ds(loff, size)],
            send_sem=hsend.at[t],
            recv_sem=hrecv,
            device_id=(p + t * prefill, c),
            device_id_type=MESH,
        )

    @pl.when(turn == 0)
    def _():
        for t, start, size, loff in segs:
            if t > 0:
                spread(t, start, size, loff).start()

    small[0].wait()
    small[1].wait()
    for h in range(hq):
        qs[pl.ds(h, rows, stride=hq), :] = qv[:, h * HD : (h + 1) * HD].astype(F32)
    for k in range(fw // HD):
        frall[pl.ds(c, 1), k] = frv[:, k * HD : (k + 1) * HD].astype(F32)[None]

    def q_copy(d, slot):
        return pltpu.make_async_remote_copy(
            src_ref=qs.at[pl.ds(pl.multiple_of(d * oh, oh), oh)],
            dst_ref=qrecv.at[slot],
            send_sem=qsend.at[d],
            recv_sem=qrsem.at[slot],
            device_id=(g, d),
            device_id_type=MESH,
        )

    def f_copy(d, slot):
        return pltpu.make_async_remote_copy(
            src_ref=frall.at[c],
            dst_ref=frall.at[slot],
            send_sem=fsend.at[d],
            recv_sem=frsem.at[slot],
            device_id=(g, d),
            device_id_type=MESH,
        )

    def send_q(o, carry):
        q_copy(peer(o), c).start()
        f_copy(peer(o), c).start()
        return carry

    lax.fori_loop(1, n, send_q, 0)
    qrecv[pl.ds(c, 1)] = qs[pl.ds(pl.multiple_of(c * oh, oh), oh), :][None]

    def rs_copy(s, d, slot):
        _, _, size, loff = segs[s]
        return pltpu.make_async_remote_copy(
            src_ref=part.at[d, pl.ds(loff, size)],
            dst_ref=rsbuf.at[slot, pl.ds(loff, size)],
            send_sem=rssend.at[s, d],
            recv_sem=rsrecv.at[s, slot],
            device_id=(g, d),
            device_id_type=MESH,
        )

    def project(s, wait_w):
        _, _, size, loff = segs[s]

        def one(o, carry):
            d = peer(o)
            if wait_w:
                for copy in w_copies(d):
                    copy.wait()
            part[d, pl.ds(loff, size), :] = jnp.dot(
                hid[pl.ds(loff, size), :], w[d], preferred_element_type=F32
            ).astype(BF16)
            rs_copy(s, d, c).start()
            return carry

        lax.fori_loop(1, n, one, 0)

    def own_part(s, wait_w):
        _, _, size, loff = segs[s]
        if wait_w:
            for copy in w_copies(c):
                copy.wait()
        return jnp.dot(hid[pl.ds(loff, size), :], w[c], preferred_element_type=F32)

    def ag_copy(s, t):
        _, start, size, _ = segs[s]
        ref = kv.at[pl.ds(start, size)]
        return pltpu.make_async_remote_copy(
            src_ref=ref,
            dst_ref=ref,
            send_sem=agsend.at[s, t],
            recv_sem=agrecv.at[s],
            device_id=(p + t * prefill, c),
            device_id_type=MESH,
        )

    def finish(s, wait_w):
        owner, start, size, loff = segs[s]
        total = own_part(s, wait_w)
        for o in range(1, n):
            src = peer(n - o)
            rs_copy(s, src, src).wait_recv()
            total = total + rsbuf[src, pl.ds(loff, size), :].astype(F32)
        kv[pl.ds(start, size), :] = total.astype(BF16)
        for t in range(1, TURNS):
            if t != owner:
                ag_copy(s, t).start()

    @pl.when(turn == 0)
    def _():
        own_hidden.wait()
        project(0, True)
        project(1, False)

    small[2].wait()
    for copy in small[4:]:
        copy.wait()
    for r in range(rows):
        for k in range(mkv.shape[0]):
            packed[k, pl.ds(r, 1), :] = mkv[k, pl.ds(states[r], 1), :]
    words = HD
    span = words * BITS
    token = lax.broadcasted_iota(jnp.int32, (words, span), 1)
    gap = token - BITS * lax.broadcasted_iota(jnp.int32, (words, span), 0)
    expand = jnp.where((gap >= 0) & (gap < BITS), 1.0, 0.0).astype(BF16)
    lane = lax.broadcasted_iota(jnp.int32, (rows, span), 1)
    lane_f = lane.astype(F32)
    bit = lane - BITS * jnp.floor((lane_f + 0.5) / BITS).astype(jnp.int32)
    shift = jnp.bitwise_and(bit, 7)
    peak = jnp.full((rows, 1), -jnp.inf, F32)
    for k in range(vdev // span):
        word = packed[k]
        pieces = jnp.concatenate(
            [
                jnp.bitwise_and(jnp.right_shift(word, 8 * i), 255).astype(F32)
                for i in range(4)
            ],
            axis=0,
        ).astype(BF16)
        got = jnp.dot(pieces, expand, preferred_element_type=F32)
        low = jnp.where(bit < 8, got[:rows], got[rows : 2 * rows])
        high = jnp.where(bit < 24, got[2 * rows : 3 * rows], got[3 * rows :])
        byte = jnp.where(bit < 16, low, high).astype(jnp.int32)
        ok = jnp.bitwise_and(jnp.right_shift(byte, shift), 1) == 1
        value = jnp.where(ok, lgv[:, k * span : (k + 1) * span].astype(F32), -jnp.inf)
        lp[:, k * span : (k + 1) * span] = value
        peak = jnp.maximum(peak, jnp.max(value, axis=1, keepdims=True))
    terms = jnp.sum(jnp.exp(lp[...] - peak), axis=1, keepdims=True)
    stat[pl.ds(c, 1), 0] = jnp.broadcast_to(peak, (rows, HD))[None]
    stat[pl.ds(c, 1), 1] = jnp.broadcast_to(terms, (rows, HD))[None]

    def s_copy(d, slot):
        return pltpu.make_async_remote_copy(
            src_ref=stat.at[c],
            dst_ref=stat.at[slot],
            send_sem=ssend.at[d],
            recv_sem=srsem.at[slot],
            device_id=(g, d),
            device_id_type=MESH,
        )

    def send_s(o, carry):
        s_copy(peer(o), c).start()
        return carry

    lax.fori_loop(1, n, send_s, 0)

    def recv_q(o, carry):
        src = peer(o)
        q_copy(src, src).wait_recv()
        f_copy(src, src).wait_recv()
        return carry

    lax.fori_loop(1, n, recv_q, 0)
    small[3].wait()
    position = lax.broadcasted_iota(jnp.int32, (1, npos), 1)

    def own_rows(i, first):
        out = []
        for h in range(KVH):
            col = first + h * HD
            row = frall[col // fw, col % fw // HD, pl.ds(c * own + i, 1), :]
            out.append(jnp.broadcast_to(row, (GQ, HD)))
        return jnp.concatenate(out, axis=0)

    for i in range(own):
        query = jnp.concatenate([qrecv[d, i * hq : (i + 1) * hq, :] for d in range(n)], axis=0)
        score = jnp.concatenate(
            [
                lax.dot_general(
                    query[h * GQ : (h + 1) * GQ].astype(BF16),
                    cv[i, :, h * HD : (h + 1) * HD],
                    (((1,), (1,)), ((), ())),
                    preferred_element_type=F32,
                )
                for h in range(KVH)
            ],
            axis=0,
        )
        score = jnp.where(position < clen[i], score * scale, -jnp.inf)
        mine = jnp.sum(query * own_rows(i, 0), axis=1, keepdims=True) * scale
        top = jnp.maximum(jnp.max(score, axis=1, keepdims=True), mine)
        expo = jnp.exp(score - top)
        mine = jnp.exp(mine - top)
        denom = jnp.sum(expo, axis=1, keepdims=True) + mine
        weight = expo / denom
        mine = (mine / denom).astype(BF16).astype(F32)
        result = jnp.concatenate(
            [
                jnp.dot(
                    weight[h * GQ : (h + 1) * GQ].astype(BF16),
                    cv[i, :, half + h * HD : half + (h + 1) * HD],
                    preferred_element_type=F32,
                )
                for h in range(KVH)
            ],
            axis=0,
        )
        result = result + mine * own_rows(i, half)
        for d in range(n):
            osend[d, i * hq : (i + 1) * hq, :] = result[d * hq : (d + 1) * hq]

    def o_copy(d, slot):
        return pltpu.make_async_remote_copy(
            src_ref=osend.at[d],
            dst_ref=orecv.at[pl.ds(pl.multiple_of(slot * oh, oh), oh)],
            send_sem=osem.at[d],
            recv_sem=orsem.at[slot],
            device_id=(g, d),
            device_id_type=MESH,
        )

    def send_o(o, carry):
        o_copy(peer(o), c).start()
        return carry

    lax.fori_loop(1, n, send_o, 0)
    orecv[pl.ds(pl.multiple_of(c * oh, oh), oh), :] = osend[c]

    for s, (owner, start, size, loff) in enumerate(segs):
        if owner > 0:

            @pl.when(turn == owner)
            def _(s=s, owner=owner, start=start, size=size, loff=loff):
                spread(owner, start, size, loff).wait_recv()
                project(s, True)

    @pl.when(turn == 0)
    def _():
        finish(0, True)
        finish(1, False)

    def recv_s(o, carry):
        src = peer(o)
        s_copy(src, src).wait_recv()
        return carry

    lax.fori_loop(1, n, recv_s, 0)
    peaks = stat[0, 0]
    for d in range(1, n):
        peaks = jnp.maximum(peaks, stat[d, 0])
    total = jnp.zeros_like(peaks)
    for d in range(n):
        total = total + stat[d, 1] * jnp.exp(stat[d, 0] - peaks)
    norm = (peaks + jnp.log(total))[:, :1]
    value = lp[...]
    lp[...] = jnp.where(value == -jnp.inf, 0.0, value - norm)
    lp_copy = pltpu.make_async_copy(lp, lp_out, lsem.at[2])
    lp_copy.start()

    line = lax.broadcasted_iota(jnp.int32, (rows, 1), 0)
    slot = lax.rem(line, own) * n + line // own
    spot = lax.broadcasted_iota(jnp.int32, (rows, block), 1)
    begin = jnp.full((rows, 1), 0, jnp.int32)
    length = jnp.full((rows, 1), 0, jnp.int32)
    at = jnp.int32(0)
    rank = jnp.int32(0)
    for k in range(plen.shape[1]):
        size = plen[p, k]
        chosen = (ostep[p, k] == turn).astype(jnp.int32)
        hit = slot == rank * chosen - (1 - chosen)
        begin = jnp.where(hit, at, begin)
        length = jnp.where(hit, size, length)
        at = at + size
        rank = rank + chosen
    landed = length > 0
    bias = jnp.where((spot >= begin) & (spot < begin + length), 0.0, -jnp.inf)

    for s, (owner, start, size, loff) in enumerate(segs):
        if owner > 0:

            @pl.when(turn == owner)
            def _(s=s):
                finish(s, True)

    def recv_o(o, carry):
        src = peer(o)
        o_copy(src, src).wait_recv()
        return carry

    lax.fori_loop(1, n, recv_o, 0)

    @pl.when(turn == 0)
    def _():
        for h in range(hq):
            att[:, h * HD : (h + 1) * HD] = orecv[pl.ds(h, rows, stride=hq), :].astype(BF16)

    @pl.when(turn > 0)
    def _():
        for s, (owner, start, size, loff) in enumerate(segs):

            @pl.when(turn != owner)
            def _(s=s):
                ag_copy(s, 0).wait_recv()

        biases = jnp.concatenate([bias] * gq, axis=0)
        for j in range(kh):
            query = jnp.concatenate(
                [
                    qv[:, (j * gq + x) * HD : (j * gq + x + 1) * HD].astype(F32)
                    for x in range(gq)
                ],
                axis=0,
            )

            def mine_of(first):
                col = first + (kv_first(c) + j) * HD
                return jnp.concatenate([frall[col // fw, lax.rem(col, fw) // HD]] * gq, axis=0)

            score = lax.dot_general(
                query.astype(BF16),
                kv[:, j * HD : (j + 1) * HD],
                (((1,), (1,)), ((), ())),
                preferred_element_type=F32,
            )
            score = score * scale + biases
            mine = jnp.sum(query * mine_of(0), axis=1, keepdims=True) * scale
            top = jnp.maximum(jnp.max(score, axis=1, keepdims=True), mine)
            expo = jnp.exp(score - top)
            mine = jnp.exp(mine - top)
            denom = jnp.sum(expo, axis=1, keepdims=True) + mine
            weight = (expo / denom).astype(BF16)
            mine = (mine / denom).astype(BF16).astype(F32)
            result = jnp.dot(
                weight, kv[:, kw + j * HD : kw + (j + 1) * HD], preferred_element_type=F32
            )
            result = result + mine * mine_of(half)
            for x in range(gq):
                h = j * gq + x
                cached = orecv[pl.ds(h, rows, stride=hq), :]
                att[:, h * HD : (h + 1) * HD] = jnp.where(
                    landed, result[x * rows : (x + 1) * rows], cached
                ).astype(BF16)

    att_copy = pltpu.make_async_copy(att, att_out, lsem.at[0])
    att_copy.start()

    def drain(o, carry):
        d = peer(o)
        q_copy(d, c).wait_send()
        f_copy(d, c).wait_send()
        s_copy(d, c).wait_send()
        o_copy(d, c).wait_send()
        return carry

    lax.fori_loop(1, n, drain, 0)

    for s, (owner, start, size, loff) in enumerate(segs):

        @pl.when(turn == owner)
        def _(s=s, owner=owner):
            def drain_rs(o, carry):
                rs_copy(s, peer(o), c).wait_send()
                return carry

            lax.fori_loop(1, n, drain_rs, 0)
            for t in range(1, TURNS):
                if t != owner:
                    ag_copy(s, t).wait_send()

    @pl.when(turn == 0)
    def _():
        for t, start, size, loff in segs:
            if t > 0:
                spread(t, start, size, loff).wait_send()

    lp_copy.wait()
    att_copy.wait()


def solution(mesh):
    n = mesh.shape["tp"]
    groups = mesh.shape["group"]

    def per_device(
        hidden, w_kv, plen, ostep, cache, clen, queries, fresh, logits, states, masks
    ):
        block, dl = hidden.shape
        rows, vdev = logits.shape
        own, npos, kvw = cache.shape
        hq = HEADS // n
        kw2 = 2 * max(1, hq // GQ) * HD
        oh = own * hq
        fw = fresh.shape[1]
        segs = segments(block)
        ns = len(segs)
        tmax = max(size + loff for _, _, size, loff in segs)
        dma = pltpu.SemaphoreType.DMA
        smem = pl.BlockSpec(memory_space=pltpu.SMEM)
        anys = pl.BlockSpec(memory_space=pl.ANY)
        return pl.pallas_call(
            functools.partial(kernel, n, groups),
            out_shape=(
                jax.ShapeDtypeStruct(queries.shape, BF16),
                jax.ShapeDtypeStruct(logits.shape, F32),
            ),
            in_specs=[smem] * 4 + [anys] * 7,
            out_specs=(anys, anys),
            scratch_shapes=[
                pltpu.VMEM((tmax, dl), BF16),
                pltpu.VMEM((n, dl, kw2), BF16),
                pltpu.VMEM((n, tmax, kw2), BF16),
                pltpu.VMEM((n, tmax, kw2), BF16),
                pltpu.VMEM((block, kw2), BF16),
                pltpu.VMEM(cache.shape, BF16),
                pltpu.VMEM(queries.shape, BF16),
                pltpu.VMEM(fresh.shape, BF16),
                pltpu.VMEM(logits.shape, BF16),
                pltpu.VMEM((masks.shape[1] // HD,) + (masks.shape[0], HD), jnp.int32),
                pltpu.VMEM((masks.shape[1] // HD, rows, HD), jnp.int32),
                pltpu.VMEM((rows * hq, HD), F32),
                pltpu.VMEM((n, oh, HD), F32),
                pltpu.VMEM((n, oh, HD), F32),
                pltpu.VMEM((rows * hq, HD), F32),
                pltpu.VMEM((n, fw // HD, rows, HD), F32),
                pltpu.VMEM((n, 2, rows, HD), F32),
                pltpu.VMEM(logits.shape, F32),
                pltpu.VMEM(queries.shape, BF16),
                dma((6 + masks.shape[1] // HD,)),
                dma((n, 2)),
                dma((TURNS,)),
                dma,
                dma((ns, n)),
                dma((ns, n)),
                dma((ns, TURNS)),
                dma((ns,)),
                dma((n,)),
                dma((n,)),
                dma((n,)),
                dma((n,)),
                dma((n,)),
                dma((n,)),
                dma((n,)),
                dma((n,)),
            ],
            compiler_params=pltpu.CompilerParams(
                collective_id=0, has_side_effects=True, vmem_limit_bytes=60 * 1024 * 1024
            ),
        )(plen, ostep, clen, states, hidden, w_kv, cache, queries, fresh, logits, masks)

    in_specs = (
        P("group", "tp"),
        P("tp", None),
        P(),
        P(),
        P(("group", "tp"), None, None),
        P(("group", "tp")),
        P("group", "tp"),
        P("group", "tp"),
        P("group", "tp"),
        P("group"),
        P(None, "tp"),
    )
    out_specs = (P("group", "tp"), P("group", "tp"))
    return jax.shard_map(
        per_device, mesh=mesh, in_specs=in_specs, out_specs=out_specs, check_vma=False
    )
```

```python
import functools
import math

import jax
import jax.numpy as jnp
from jax import lax
from jax.experimental import pallas as pl
from jax.experimental.pallas import tpu as pltpu
from jax.sharding import PartitionSpec as P

HEADS = 64
KVH = 8
HD = 128
GQ = HEADS // KVH
TURNS = 4
BITS = 30
PLAN = ((0, 3), (0, 3), (1, 2), (2, 2), (3, 2), (2, 2), (1, 1), (3, 1))
MESH = pl.DeviceIdType.MESH
F32 = jnp.float32
BF16 = jnp.bfloat16


def segments(block):
    out, filled, at = [], [0] * TURNS, 0
    for owner, share in PLAN:
        size = block * share // 16
        out.append((owner, at, size, filled[owner]))
        filled[owner] += size
        at += size
    return tuple(out)


def kernel(
    n, groups,
    plen_in, ostep_in, clen_in, states_in, hidden, w_kv, cache, queries, fresh, logits, masks,
    att, lp,
    plen, ostep, clen, states,
    hid, w, part, rsbuf, kv, cv, qv, fb, lgv, mkv, packed, qs, qb, qrecv, osend, orecv, of,
    frall, stat,
    lsem, wsem, hsend, hrecv, rssend, rsrecv, agsend, agrecv,
    csem, qsend, qrsem, fsend, frsem, osem, orsem, ssend, srsem,
):
    g = lax.axis_index("group")
    c = lax.axis_index("tp")
    prefill = groups // TURNS
    p = lax.rem(g, prefill)
    turn = g // prefill
    block, dl = hidden.shape
    rows, vdev = logits.shape
    own = cache.shape[0]
    npos = cache.shape[1]
    hq = HEADS // n
    gq = min(GQ, hq)
    kh = max(1, hq // GQ)
    kw = kh * HD
    oh = own * hq
    fw = fresh.shape[1]
    half = KVH * HD
    segs = segments(block)
    scale = 1.0 / math.sqrt(HD)

    def peer(o):
        return lax.rem(c + o, n)

    def kv_first(d):
        return (d * hq) // GQ

    barrier = pltpu.get_barrier_semaphore()

    def hello(o, carry):
        pl.semaphore_signal(barrier, inc=1, device_id=(g, peer(o)), device_id_type=MESH)
        return carry

    lax.fori_loop(1, n, hello, 0)
    for o in range(1, TURNS):
        pl.semaphore_signal(
            barrier, inc=1, device_id=(lax.rem(g + o * prefill, groups), c), device_id_type=MESH
        )

    small = [
        pltpu.make_async_copy(src, dst, lsem.at[i])
        for i, (src, dst) in enumerate(
            ((queries, qv), (fresh, fb.at[c]), (logits, lgv), (cache, cv))
        )
    ]
    small += [
        pltpu.make_async_copy(masks.at[:, k * HD : (k + 1) * HD], mkv.at[k], lsem.at[6 + k])
        for k in range(mkv.shape[0])
    ]
    scalars = [
        pltpu.make_async_copy(src, dst, csem.at[i])
        for i, (src, dst) in enumerate(
            ((plen_in, plen), (ostep_in, ostep), (clen_in, clen), (states_in, states))
        )
    ]
    own_tokens = sum(size for owner, _, size, _ in segs if owner == 0)
    own_hidden = pltpu.make_async_copy(
        hidden.at[pl.ds(0, own_tokens)], hid.at[pl.ds(0, own_tokens)], lsem.at[5]
    )

    def w_copies(d):
        first = pl.multiple_of(kv_first(d) * HD, HD)
        return [
            pltpu.make_async_copy(
                w_kv.at[:, pl.ds(pl.multiple_of(first + s * half, HD), kw)],
                w.at[d, :, pl.ds(s * kw, kw)],
                wsem.at[d, s],
            )
            for s in range(2)
        ]

    small[0].start()
    small[1].start()
    for copy in scalars:
        copy.start()

    @pl.when(turn == 0)
    def _():
        own_hidden.start()

    def start_w(o, carry):
        for copy in w_copies(peer(o)):
            copy.start()
        return carry

    lax.fori_loop(1, n, start_w, 0)
    for copy in small[2:]:
        copy.start()
    start_w(0, 0)

    small[0].wait()
    for h in range(hq):
        qs[pl.ds(h, rows, stride=hq), :] = qv[:, h * HD : (h + 1) * HD].astype(F32)
    for d in range(n):
        qb[d] = qs[d * oh : (d + 1) * oh, :].astype(BF16)
    pl.semaphore_wait(barrier, n - 1 + TURNS - 1)

    def spread(s):
        t, start, size, loff = segs[s]
        return pltpu.make_async_remote_copy(
            src_ref=hidden.at[pl.ds(start, size)],
            dst_ref=hid.at[pl.ds(loff, size)],
            send_sem=hsend.at[s],
            recv_sem=hrecv.at[s],
            device_id=(p + t * prefill, c),
            device_id_type=MESH,
        )

    @pl.when(turn == 0)
    def _():
        for s, seg in enumerate(segs):
            if seg[0] > 0:
                spread(s).start()

    def q_copy(d, slot):
        return pltpu.make_async_remote_copy(
            src_ref=qb.at[d],
            dst_ref=qrecv.at[slot],
            send_sem=qsend.at[d],
            recv_sem=qrsem.at[slot],
            device_id=(g, d),
            device_id_type=MESH,
        )

    def f_copy(d, slot):
        return pltpu.make_async_remote_copy(
            src_ref=fresh,
            dst_ref=fb.at[slot],
            send_sem=fsend.at[d],
            recv_sem=frsem.at[slot],
            device_id=(g, d),
            device_id_type=MESH,
        )

    def send_q(o, carry):
        q_copy(peer(o), c).start()
        f_copy(peer(o), c).start()
        return carry

    lax.fori_loop(1, n, send_q, 0)
    qrecv[pl.ds(c, 1)] = qb[pl.ds(c, 1)]

    def rs_copy(s, d, slot):
        _, _, size, loff = segs[s]
        return pltpu.make_async_remote_copy(
            src_ref=part.at[d, pl.ds(loff, size)],
            dst_ref=rsbuf.at[slot, pl.ds(loff, size)],
            send_sem=rssend.at[s, d],
            recv_sem=rsrecv.at[s, slot],
            device_id=(g, d),
            device_id_type=MESH,
        )

    def project(s, wait_w):
        _, _, size, loff = segs[s]

        def one(o, carry):
            d = peer(o)
            if wait_w:
                for copy in w_copies(d):
                    copy.wait()
            part[d, pl.ds(loff, size), :] = jnp.dot(
                hid[pl.ds(loff, size), :], w[d], preferred_element_type=F32
            ).astype(BF16)
            rs_copy(s, d, c).start()
            return carry

        lax.fori_loop(1, n, one, 0)

    def own_part(s, wait_w):
        _, _, size, loff = segs[s]
        if wait_w:
            for copy in w_copies(c):
                copy.wait()
        return jnp.dot(hid[pl.ds(loff, size), :], w[c], preferred_element_type=F32)

    def ag_copy(s, t):
        _, start, size, _ = segs[s]
        ref = kv.at[pl.ds(start, size)]
        return pltpu.make_async_remote_copy(
            src_ref=ref,
            dst_ref=ref,
            send_sem=agsend.at[s, t],
            recv_sem=agrecv.at[s],
            device_id=(p + t * prefill, c),
            device_id_type=MESH,
        )

    def finish(s, wait_w):
        owner, start, size, loff = segs[s]
        total = own_part(s, wait_w)
        for o in range(1, n):
            src = peer(n - o)
            rs_copy(s, src, src).wait_recv()
            total = total + rsbuf[src, pl.ds(loff, size), :].astype(F32)
        kv[pl.ds(start, size), :] = total.astype(BF16)
        for t in range(1, TURNS):
            if t != owner:
                ag_copy(s, t).start()

    @pl.when(turn == 0)
    def _():
        own_hidden.wait()
        for s, seg in enumerate(segs):
            if seg[0] == 0:
                project(s, seg[3] == 0)

    small[2].wait()
    for copy in small[4:]:
        copy.wait()
    for copy in scalars:
        copy.wait()
    for r in range(rows):
        for k in range(mkv.shape[0]):
            packed[k, pl.ds(r, 1), :] = mkv[k, pl.ds(states[r], 1), :]
    words = HD
    span = words * BITS
    token = lax.broadcasted_iota(jnp.int32, (words, span), 1)
    gap = token - BITS * lax.broadcasted_iota(jnp.int32, (words, span), 0)
    expand = jnp.where((gap >= 0) & (gap < BITS), 1.0, 0.0).astype(BF16)
    lane = lax.broadcasted_iota(jnp.int32, (rows, span), 1)
    lane_f = lane.astype(F32)
    bit = lane - BITS * jnp.floor((lane_f + 0.5) / BITS).astype(jnp.int32)
    shift = jnp.bitwise_and(bit, 7)
    peak = jnp.full((rows, 1), -jnp.inf, F32)
    for k in range(vdev // span):
        word = packed[k]
        pieces = jnp.concatenate(
            [
                jnp.bitwise_and(jnp.right_shift(word, 8 * i), 255).astype(F32)
                for i in range(4)
            ],
            axis=0,
        ).astype(BF16)
        got = jnp.dot(pieces, expand, preferred_element_type=F32)
        low = jnp.where(bit < 8, got[:rows], got[rows : 2 * rows])
        high = jnp.where(bit < 24, got[2 * rows : 3 * rows], got[3 * rows :])
        byte = jnp.where(bit < 16, low, high).astype(jnp.int32)
        ok = jnp.bitwise_and(jnp.right_shift(byte, shift), 1) == 1
        value = jnp.where(ok, lgv[:, k * span : (k + 1) * span].astype(F32), -jnp.inf)
        lp[:, k * span : (k + 1) * span] = value
        peak = jnp.maximum(peak, jnp.max(value, axis=1, keepdims=True))
    terms = jnp.sum(jnp.exp(lp[...] - peak), axis=1, keepdims=True)
    side = lax.broadcasted_iota(jnp.int32, (rows, HD), 1) < HD // 2
    stat[pl.ds(c, 1)] = jnp.where(side, peak, terms)[None]

    def s_copy(d, slot):
        return pltpu.make_async_remote_copy(
            src_ref=stat.at[c],
            dst_ref=stat.at[slot],
            send_sem=ssend.at[d],
            recv_sem=srsem.at[slot],
            device_id=(g, d),
            device_id_type=MESH,
        )

    def send_s(o, carry):
        s_copy(peer(o), c).start()
        return carry

    lax.fori_loop(1, n, send_s, 0)

    def recv_q(o, carry):
        src = peer(o)
        q_copy(src, src).wait_recv()
        f_copy(src, src).wait_recv()
        return carry

    lax.fori_loop(1, n, recv_q, 0)
    small[1].wait()
    for d in range(n):
        for k in range(fw // HD):
            frall[d, k] = fb[d, :, k * HD : (k + 1) * HD].astype(F32)
    small[3].wait()
    position = lax.broadcasted_iota(jnp.int32, (1, npos), 1)

    def own_rows(i, first):
        out = []
        for h in range(KVH):
            col = first + h * HD
            row = frall[col // fw, col % fw // HD, pl.ds(c * own + i, 1), :]
            out.append(jnp.broadcast_to(row, (GQ, HD)))
        return jnp.concatenate(out, axis=0)

    arrived = [qrecv[d].astype(F32) for d in range(n)]
    results = []
    for i in range(own):
        query = jnp.concatenate([x[i * hq : (i + 1) * hq] for x in arrived], axis=0)
        score = jnp.concatenate(
            [
                lax.dot_general(
                    query[h * GQ : (h + 1) * GQ].astype(BF16),
                    cv[i, :, h * HD : (h + 1) * HD],
                    (((1,), (1,)), ((), ())),
                    preferred_element_type=F32,
                )
                for h in range(KVH)
            ],
            axis=0,
        )
        score = jnp.where(position < clen[i], score * scale, -jnp.inf)
        mine = jnp.sum(query * own_rows(i, 0), axis=1, keepdims=True) * scale
        top = jnp.maximum(jnp.max(score, axis=1, keepdims=True), mine)
        expo = jnp.exp(score - top)
        mine = jnp.exp(mine - top)
        denom = jnp.sum(expo, axis=1, keepdims=True) + mine
        weight = expo / denom
        mine = (mine / denom).astype(BF16).astype(F32)
        result = jnp.concatenate(
            [
                jnp.dot(
                    weight[h * GQ : (h + 1) * GQ].astype(BF16),
                    cv[i, :, half + h * HD : half + (h + 1) * HD],
                    preferred_element_type=F32,
                )
                for h in range(KVH)
            ],
            axis=0,
        )
        results.append(result + mine * own_rows(i, half))
    for d in range(n):
        osend[d] = jnp.concatenate([x[d * hq : (d + 1) * hq] for x in results], axis=0).astype(BF16)

    def o_copy(d, slot):
        return pltpu.make_async_remote_copy(
            src_ref=osend.at[d],
            dst_ref=orecv.at[slot],
            send_sem=osem.at[d],
            recv_sem=orsem.at[slot],
            device_id=(g, d),
            device_id_type=MESH,
        )

    def send_o(o, carry):
        o_copy(peer(o), c).start()
        return carry

    lax.fori_loop(1, n, send_o, 0)
    orecv[pl.ds(c, 1)] = osend[pl.ds(c, 1)]

    for s, (owner, start, size, loff) in enumerate(segs):
        if owner > 0:

            @pl.when(turn == owner)
            def _(s=s, owner=owner, start=start, size=size, loff=loff):
                spread(s).wait_recv()
                project(s, loff == 0)

    @pl.when(turn == 0)
    def _():
        for s, seg in enumerate(segs):
            if seg[0] == 0:
                finish(s, seg[3] == 0)

    def recv_s(o, carry):
        src = peer(o)
        s_copy(src, src).wait_recv()
        return carry

    lax.fori_loop(1, n, recv_s, 0)
    peaks = stat[0][:, :1]
    for d in range(1, n):
        peaks = jnp.maximum(peaks, stat[d][:, :1])
    total = jnp.zeros_like(peaks)
    for d in range(n):
        total = total + stat[d][:, HD // 2 : HD // 2 + 1] * jnp.exp(stat[d][:, :1] - peaks)
    norm = peaks + jnp.log(total)
    value = lp[...]
    lp[...] = jnp.where(value == -jnp.inf, 0.0, value - norm)

    line = lax.broadcasted_iota(jnp.int32, (rows, 1), 0)
    slot = lax.rem(line, own) * n + line // own
    spot = lax.broadcasted_iota(jnp.int32, (rows, block), 1)
    begin = jnp.full((rows, 1), 0, jnp.int32)
    length = jnp.full((rows, 1), 0, jnp.int32)
    at = jnp.int32(0)
    rank = jnp.int32(0)
    for k in range(plen.shape[1]):
        size = plen[p, k]
        chosen = (ostep[p, k] == turn).astype(jnp.int32)
        hit = slot == rank * chosen - (1 - chosen)
        begin = jnp.where(hit, at, begin)
        length = jnp.where(hit, size, length)
        at = at + size
        rank = rank + chosen
    landed = length > 0
    bias = jnp.where((spot >= begin) & (spot < begin + length), 0.0, -jnp.inf)

    for s, (owner, start, size, loff) in enumerate(segs):
        if owner > 0:

            @pl.when(turn == owner)
            def _(s=s, loff=loff):
                finish(s, loff == 0)

    def recv_o(o, carry):
        src = peer(o)
        o_copy(src, src).wait_recv()
        return carry

    lax.fori_loop(1, n, recv_o, 0)
    for d in range(n):
        of[d * oh : (d + 1) * oh, :] = orecv[d].astype(F32)

    @pl.when(turn == 0)
    def _():
        for h in range(hq):
            att[:, h * HD : (h + 1) * HD] = of[pl.ds(h, rows, stride=hq), :].astype(BF16)

    @pl.when(turn > 0)
    def _():
        for s, (owner, start, size, loff) in enumerate(segs):

            @pl.when(turn != owner)
            def _(s=s):
                ag_copy(s, 0).wait_recv()

        biases = jnp.concatenate([bias] * gq, axis=0)
        for j in range(kh):
            query = jnp.concatenate(
                [
                    qv[:, (j * gq + x) * HD : (j * gq + x + 1) * HD].astype(F32)
                    for x in range(gq)
                ],
                axis=0,
            )

            def mine_of(first):
                col = first + (kv_first(c) + j) * HD
                return jnp.concatenate([frall[col // fw, lax.rem(col, fw) // HD]] * gq, axis=0)

            score = lax.dot_general(
                query.astype(BF16),
                kv[:, j * HD : (j + 1) * HD],
                (((1,), (1,)), ((), ())),
                preferred_element_type=F32,
            )
            score = score * scale + biases
            mine = jnp.sum(query * mine_of(0), axis=1, keepdims=True) * scale
            top = jnp.maximum(jnp.max(score, axis=1, keepdims=True), mine)
            expo = jnp.exp(score - top)
            mine = jnp.exp(mine - top)
            denom = jnp.sum(expo, axis=1, keepdims=True) + mine
            weight = (expo / denom).astype(BF16)
            mine = (mine / denom).astype(BF16).astype(F32)
            result = jnp.dot(
                weight, kv[:, kw + j * HD : kw + (j + 1) * HD], preferred_element_type=F32
            )
            result = result + mine * mine_of(half)
            for x in range(gq):
                h = j * gq + x
                cached = of[pl.ds(h, rows, stride=hq), :]
                att[:, h * HD : (h + 1) * HD] = jnp.where(
                    landed, result[x * rows : (x + 1) * rows], cached
                ).astype(BF16)


    def drain(o, carry):
        d = peer(o)
        q_copy(d, c).wait_send()
        f_copy(d, c).wait_send()
        s_copy(d, c).wait_send()
        o_copy(d, c).wait_send()
        return carry

    lax.fori_loop(1, n, drain, 0)

    for s, (owner, start, size, loff) in enumerate(segs):

        @pl.when(turn == owner)
        def _(s=s, owner=owner):
            def drain_rs(o, carry):
                rs_copy(s, peer(o), c).wait_send()
                return carry

            lax.fori_loop(1, n, drain_rs, 0)
            for t in range(1, TURNS):
                if t != owner:
                    ag_copy(s, t).wait_send()

    @pl.when(turn == 0)
    def _():
        for s, seg in enumerate(segs):
            if seg[0] > 0:
                spread(s).wait_send()


def solution(mesh):
    n = mesh.shape["tp"]
    groups = mesh.shape["group"]

    def per_device(
        hidden, w_kv, plen, ostep, cache, clen, queries, fresh, logits, states, masks
    ):
        block, dl = hidden.shape
        rows, vdev = logits.shape
        own, npos, kvw = cache.shape
        hq = HEADS // n
        kw2 = 2 * max(1, hq // GQ) * HD
        oh = own * hq
        fw = fresh.shape[1]
        segs = segments(block)
        ns = len(segs)
        tmax = max(size + loff for _, _, size, loff in segs)
        dma = pltpu.SemaphoreType.DMA
        vmem = pl.BlockSpec(memory_space=pltpu.VMEM)
        anys = pl.BlockSpec(memory_space=pl.ANY)
        made = pl.pallas_call(
            functools.partial(kernel, n, groups),
            out_shape=(
                pltpu.VMEM(queries.shape, BF16),
                pltpu.VMEM(logits.shape, F32),
            ),
            in_specs=[anys] * 11,
            out_specs=(vmem, vmem),
            scratch_shapes=[pltpu.SMEM(x.shape, jnp.int32) for x in (plen, ostep, clen, states)]
            + [
                pltpu.VMEM((tmax, dl), BF16),
                pltpu.VMEM((n, dl, kw2), BF16),
                pltpu.VMEM((n, tmax, kw2), BF16),
                pltpu.VMEM((n, tmax, kw2), BF16),
                pltpu.VMEM((block, kw2), BF16),
                pltpu.VMEM(cache.shape, BF16),
                pltpu.VMEM(queries.shape, BF16),
                pltpu.VMEM((n, rows, fw), BF16),
                pltpu.VMEM(logits.shape, BF16),
                pltpu.VMEM((masks.shape[1] // HD,) + (masks.shape[0], HD), jnp.int32),
                pltpu.VMEM((masks.shape[1] // HD, rows, HD), jnp.int32),
                pltpu.VMEM((rows * hq, HD), F32),
                pltpu.VMEM((n, oh, HD), BF16),
                pltpu.VMEM((n, oh, HD), BF16),
                pltpu.VMEM((n, oh, HD), BF16),
                pltpu.VMEM((n, oh, HD), BF16),
                pltpu.VMEM((rows * hq, HD), F32),
                pltpu.VMEM((n, fw // HD, rows, HD), F32),
                pltpu.VMEM((n, rows, HD), F32),
                dma((6 + masks.shape[1] // HD,)),
                dma((n, 2)),
                dma((ns,)),
                dma((ns,)),
                dma((ns, n)),
                dma((ns, n)),
                dma((ns, TURNS)),
                dma((ns,)),
                dma((4,)),
                dma((n,)),
                dma((n,)),
                dma((n,)),
                dma((n,)),
                dma((n,)),
                dma((n,)),
                dma((n,)),
                dma((n,)),
            ],
            compiler_params=pltpu.CompilerParams(
                collective_id=0, has_side_effects=True, vmem_limit_bytes=60 * 1024 * 1024
            ),
        )(plen, ostep, clen, states, hidden, w_kv, cache, queries, fresh, logits, masks)
        return tuple(made)

    in_specs = (
        P("group", "tp"),
        P("tp", None),
        P(),
        P(),
        P(("group", "tp"), None, None),
        P(("group", "tp")),
        P("group", "tp"),
        P("group", "tp"),
        P("group", "tp"),
        P("group"),
        P(None, "tp"),
    )
    out_specs = (P("group", "tp"), P("group", "tp"))
    return jax.shard_map(
        per_device, mesh=mesh, in_specs=in_specs, out_specs=out_specs, check_vma=False
    )
```

```python
import functools
import math

import jax
import jax.numpy as jnp
from jax import lax
from jax.experimental import pallas as pl
from jax.experimental.pallas import tpu as pltpu
from jax.sharding import PartitionSpec as P

HEADS = 64
KVH = 8
HD = 128
GQ = HEADS // KVH
TURNS = 4
BITS = 30
PLAN = ((0, 4), (0, 3), (3, 1), (2, 2), (3, 1), (2, 2), (1, 2), (1, 1))
MESH = pl.DeviceIdType.MESH
F32 = jnp.float32
BF16 = jnp.bfloat16


def segments(block):
    out, filled, at = [], [0] * TURNS, 0
    for owner, share in PLAN:
        size = block * share // 16
        out.append((owner, at, size, filled[owner]))
        filled[owner] += size
        at += size
    return tuple(out)


def kernel(
    n, groups,
    plen_in, ostep_in, clen_in, states_in, hidden, w_kv, cache, queries, fresh, logits, masks,
    att, lp,
    plen, ostep, clen, states,
    hid, w, part, rsbuf, kv, cv, qv, fb, lgv, mkv, packed, qs, qb, qrecv, osend, orecv, of,
    frall, stat,
    lsem, wsem, hsend, hrecv, rssend, rsrecv, agsend, agrecv,
    csem, qsend, qrsem, fsend, frsem, osem, orsem, ssend, srsem,
):
    g = lax.axis_index("group")
    c = lax.axis_index("tp")
    prefill = groups // TURNS
    p = lax.rem(g, prefill)
    turn = g // prefill
    block, dl = hidden.shape
    rows, vdev = logits.shape
    own = cache.shape[0]
    npos = cache.shape[1]
    hq = HEADS // n
    gq = min(GQ, hq)
    kh = max(1, hq // GQ)
    kw = kh * HD
    oh = own * hq
    fw = fresh.shape[1]
    half = KVH * HD
    segs = segments(block)
    scale = 1.0 / math.sqrt(HD)

    def peer(o):
        return lax.rem(c + o, n)

    def kv_first(d):
        return (d * hq) // GQ

    barrier = pltpu.get_barrier_semaphore()

    def hello(o, carry):
        pl.semaphore_signal(barrier, inc=1, device_id=(g, peer(o)), device_id_type=MESH)
        return carry

    lax.fori_loop(1, n, hello, 0)
    for o in range(1, TURNS):
        pl.semaphore_signal(
            barrier, inc=1, device_id=(lax.rem(g + o * prefill, groups), c), device_id_type=MESH
        )

    small = [
        pltpu.make_async_copy(src, dst, lsem.at[i])
        for i, (src, dst) in enumerate(
            ((queries, qv), (fresh, fb.at[c]), (logits, lgv), (cache, cv))
        )
    ]
    small += [
        pltpu.make_async_copy(masks.at[:, k * HD : (k + 1) * HD], mkv.at[k], lsem.at[6 + k])
        for k in range(mkv.shape[0])
    ]
    scalars = [
        pltpu.make_async_copy(src, dst, csem.at[i])
        for i, (src, dst) in enumerate(
            ((plen_in, plen), (ostep_in, ostep), (clen_in, clen), (states_in, states))
        )
    ]
    own_tokens = sum(size for owner, _, size, _ in segs if owner == 0)
    own_hidden = pltpu.make_async_copy(
        hidden.at[pl.ds(0, own_tokens)], hid.at[pl.ds(0, own_tokens)], lsem.at[5]
    )

    def w_copies(d):
        first = pl.multiple_of(kv_first(d) * HD, HD)
        return [
            pltpu.make_async_copy(
                w_kv.at[:, pl.ds(pl.multiple_of(first + s * half, HD), kw)],
                w.at[d, :, pl.ds(s * kw, kw)],
                wsem.at[d, s],
            )
            for s in range(2)
        ]

    small[0].start()
    small[1].start()
    for copy in scalars:
        copy.start()

    @pl.when(turn == 0)
    def _():
        own_hidden.start()

    def start_w(o, carry):
        for copy in w_copies(peer(o)):
            copy.start()
        return carry

    lax.fori_loop(1, n, start_w, 0)
    for copy in small[2:]:
        copy.start()
    start_w(0, 0)

    small[0].wait()
    for h in range(hq):
        qs[pl.ds(h, rows, stride=hq), :] = qv[:, h * HD : (h + 1) * HD].astype(F32)
    for d in range(n):
        qb[d] = qs[d * oh : (d + 1) * oh, :].astype(BF16)
    pl.semaphore_wait(barrier, n - 1 + TURNS - 1)

    def spread(s):
        t, start, size, loff = segs[s]
        return pltpu.make_async_remote_copy(
            src_ref=hidden.at[pl.ds(start, size)],
            dst_ref=hid.at[pl.ds(loff, size)],
            send_sem=hsend.at[s],
            recv_sem=hrecv.at[s],
            device_id=(p + t * prefill, c),
            device_id_type=MESH,
        )

    @pl.when(turn == 0)
    def _():
        for s, seg in enumerate(segs):
            if seg[0] > 0:
                spread(s).start()

    def q_copy(d, slot):
        return pltpu.make_async_remote_copy(
            src_ref=qb.at[d],
            dst_ref=qrecv.at[slot],
            send_sem=qsend.at[d],
            recv_sem=qrsem.at[slot],
            device_id=(g, d),
            device_id_type=MESH,
        )

    def f_copy(d, slot):
        return pltpu.make_async_remote_copy(
            src_ref=fresh,
            dst_ref=fb.at[slot],
            send_sem=fsend.at[d],
            recv_sem=frsem.at[slot],
            device_id=(g, d),
            device_id_type=MESH,
        )

    def send_q(o, carry):
        q_copy(peer(o), c).start()
        f_copy(peer(o), c).start()
        return carry

    lax.fori_loop(1, n, send_q, 0)
    qrecv[pl.ds(c, 1)] = qb[pl.ds(c, 1)]

    def rs_copy(s, d, slot):
        _, _, size, loff = segs[s]
        return pltpu.make_async_remote_copy(
            src_ref=part.at[d, pl.ds(loff, size)],
            dst_ref=rsbuf.at[slot, pl.ds(loff, size)],
            send_sem=rssend.at[s, d],
            recv_sem=rsrecv.at[s, slot],
            device_id=(g, d),
            device_id_type=MESH,
        )

    def project(s, wait_w):
        _, _, size, loff = segs[s]

        def one(o, carry):
            d = peer(o)
            if wait_w:
                for copy in w_copies(d):
                    copy.wait()
            part[d, pl.ds(loff, size), :] = jnp.dot(
                hid[pl.ds(loff, size), :], w[d], preferred_element_type=F32
            ).astype(BF16)
            rs_copy(s, d, c).start()
            return carry

        lax.fori_loop(1, n, one, 0)

    def own_part(s, wait_w):
        _, _, size, loff = segs[s]
        if wait_w:
            for copy in w_copies(c):
                copy.wait()
        return jnp.dot(hid[pl.ds(loff, size), :], w[c], preferred_element_type=F32)

    def ag_copy(s, t):
        _, start, size, _ = segs[s]
        ref = kv.at[pl.ds(start, size)]
        return pltpu.make_async_remote_copy(
            src_ref=ref,
            dst_ref=ref,
            send_sem=agsend.at[s, t],
            recv_sem=agrecv.at[s],
            device_id=(p + t * prefill, c),
            device_id_type=MESH,
        )

    def finish(s, wait_w):
        owner, start, size, loff = segs[s]
        total = own_part(s, wait_w)
        for o in range(1, n):
            src = peer(n - o)
            rs_copy(s, src, src).wait_recv()
            total = total + rsbuf[src, pl.ds(loff, size), :].astype(F32)
        kv[pl.ds(start, size), :] = total.astype(BF16)
        for t in range(1, TURNS):
            if t != owner:
                ag_copy(s, t).start()

    @pl.when(turn == 0)
    def _():
        own_hidden.wait()
        for s, seg in enumerate(segs):
            if seg[0] == 0:
                project(s, seg[3] == 0)

    small[2].wait()
    for copy in small[4:]:
        copy.wait()
    for copy in scalars:
        copy.wait()
    for r in range(rows):
        for k in range(mkv.shape[0]):
            packed[k, pl.ds(r, 1), :] = mkv[k, pl.ds(states[r], 1), :]
    words = HD
    span = words * BITS
    token = lax.broadcasted_iota(jnp.int32, (words, span), 1)
    gap = token - BITS * lax.broadcasted_iota(jnp.int32, (words, span), 0)
    expand = jnp.where((gap >= 0) & (gap < BITS), 1.0, 0.0).astype(BF16)
    lane = lax.broadcasted_iota(jnp.int32, (rows, span), 1)
    lane_f = lane.astype(F32)
    bit = lane - BITS * jnp.floor((lane_f + 0.5) / BITS).astype(jnp.int32)
    shift = jnp.bitwise_and(bit, 7)
    peak = jnp.full((rows, 1), -jnp.inf, F32)
    for k in range(vdev // span):
        word = packed[k]
        pieces = jnp.concatenate(
            [
                jnp.bitwise_and(jnp.right_shift(word, 8 * i), 255).astype(F32)
                for i in range(4)
            ],
            axis=0,
        ).astype(BF16)
        got = jnp.dot(pieces, expand, preferred_element_type=F32)
        low = jnp.where(bit < 8, got[:rows], got[rows : 2 * rows])
        high = jnp.where(bit < 24, got[2 * rows : 3 * rows], got[3 * rows :])
        byte = jnp.where(bit < 16, low, high).astype(jnp.int32)
        ok = jnp.bitwise_and(jnp.right_shift(byte, shift), 1) == 1
        value = jnp.where(ok, lgv[:, k * span : (k + 1) * span].astype(F32), -jnp.inf)
        lp[:, k * span : (k + 1) * span] = value
        peak = jnp.maximum(peak, jnp.max(value, axis=1, keepdims=True))
    terms = jnp.sum(jnp.exp(lp[...] - peak), axis=1, keepdims=True)
    side = lax.broadcasted_iota(jnp.int32, (rows, HD), 1) < HD // 2
    stat[pl.ds(c, 1)] = jnp.where(side, peak, terms)[None]

    def s_copy(d, slot):
        return pltpu.make_async_remote_copy(
            src_ref=stat.at[c],
            dst_ref=stat.at[slot],
            send_sem=ssend.at[d],
            recv_sem=srsem.at[slot],
            device_id=(g, d),
            device_id_type=MESH,
        )

    def send_s(o, carry):
        s_copy(peer(o), c).start()
        return carry

    lax.fori_loop(1, n, send_s, 0)

    def recv_q(o, carry):
        src = peer(o)
        q_copy(src, src).wait_recv()
        f_copy(src, src).wait_recv()
        return carry

    lax.fori_loop(1, n, recv_q, 0)
    small[1].wait()
    for d in range(n):
        for k in range(fw // HD):
            frall[d, k] = fb[d, :, k * HD : (k + 1) * HD].astype(F32)
    small[3].wait()
    position = lax.broadcasted_iota(jnp.int32, (1, npos), 1)

    def own_rows(i, first):
        out = []
        for h in range(KVH):
            col = first + h * HD
            row = frall[col // fw, col % fw // HD, pl.ds(c * own + i, 1), :]
            out.append(jnp.broadcast_to(row, (GQ, HD)))
        return jnp.concatenate(out, axis=0)

    arrived = [qrecv[d].astype(F32) for d in range(n)]
    results = []
    for i in range(own):
        query = jnp.concatenate([x[i * hq : (i + 1) * hq] for x in arrived], axis=0)
        score = jnp.concatenate(
            [
                lax.dot_general(
                    query[h * GQ : (h + 1) * GQ].astype(BF16),
                    cv[i, :, h * HD : (h + 1) * HD],
                    (((1,), (1,)), ((), ())),
                    preferred_element_type=F32,
                )
                for h in range(KVH)
            ],
            axis=0,
        )
        score = jnp.where(position < clen[i], score * scale, -jnp.inf)
        mine = jnp.sum(query * own_rows(i, 0), axis=1, keepdims=True) * scale
        top = jnp.maximum(jnp.max(score, axis=1, keepdims=True), mine)
        expo = jnp.exp(score - top)
        mine = jnp.exp(mine - top)
        denom = jnp.sum(expo, axis=1, keepdims=True) + mine
        weight = expo / denom
        mine = (mine / denom).astype(BF16).astype(F32)
        result = jnp.concatenate(
            [
                jnp.dot(
                    weight[h * GQ : (h + 1) * GQ].astype(BF16),
                    cv[i, :, half + h * HD : half + (h + 1) * HD],
                    preferred_element_type=F32,
                )
                for h in range(KVH)
            ],
            axis=0,
        )
        results.append(result + mine * own_rows(i, half))
    for d in range(n):
        osend[d] = jnp.concatenate([x[d * hq : (d + 1) * hq] for x in results], axis=0).astype(BF16)

    def o_copy(d, slot):
        return pltpu.make_async_remote_copy(
            src_ref=osend.at[d],
            dst_ref=orecv.at[slot],
            send_sem=osem.at[d],
            recv_sem=orsem.at[slot],
            device_id=(g, d),
            device_id_type=MESH,
        )

    def send_o(o, carry):
        o_copy(peer(o), c).start()
        return carry

    lax.fori_loop(1, n, send_o, 0)
    orecv[pl.ds(c, 1)] = osend[pl.ds(c, 1)]

    for s, (owner, start, size, loff) in enumerate(segs):
        if owner > 0:

            @pl.when(turn == owner)
            def _(s=s, owner=owner, start=start, size=size, loff=loff):
                spread(s).wait_recv()
                project(s, loff == 0)

    @pl.when(turn == 0)
    def _():
        for s, seg in enumerate(segs):
            if seg[0] == 0:
                finish(s, seg[3] == 0)

    def recv_s(o, carry):
        src = peer(o)
        s_copy(src, src).wait_recv()
        return carry

    lax.fori_loop(1, n, recv_s, 0)
    peaks = stat[0][:, :1]
    for d in range(1, n):
        peaks = jnp.maximum(peaks, stat[d][:, :1])
    total = jnp.zeros_like(peaks)
    for d in range(n):
        total = total + stat[d][:, HD // 2 : HD // 2 + 1] * jnp.exp(stat[d][:, :1] - peaks)
    norm = peaks + jnp.log(total)
    value = lp[...]
    lp[...] = jnp.where(value == -jnp.inf, 0.0, value - norm)

    line = lax.broadcasted_iota(jnp.int32, (rows, 1), 0)
    slot = lax.rem(line, own) * n + line // own
    spot = lax.broadcasted_iota(jnp.int32, (rows, block), 1)
    begin = jnp.full((rows, 1), 0, jnp.int32)
    length = jnp.full((rows, 1), 0, jnp.int32)
    at = jnp.int32(0)
    rank = jnp.int32(0)
    for k in range(plen.shape[1]):
        size = plen[p, k]
        chosen = (ostep[p, k] == turn).astype(jnp.int32)
        hit = slot == rank * chosen - (1 - chosen)
        begin = jnp.where(hit, at, begin)
        length = jnp.where(hit, size, length)
        at = at + size
        rank = rank + chosen
    landed = length > 0
    bias = jnp.where((spot >= begin) & (spot < begin + length), 0.0, -jnp.inf)

    for s, (owner, start, size, loff) in enumerate(segs):
        if owner > 0:

            @pl.when(turn == owner)
            def _(s=s, loff=loff):
                finish(s, loff == 0)

    def recv_o(o, carry):
        src = peer(o)
        o_copy(src, src).wait_recv()
        return carry

    lax.fori_loop(1, n, recv_o, 0)
    for d in range(n):
        of[d * oh : (d + 1) * oh, :] = orecv[d].astype(F32)

    @pl.when(turn == 0)
    def _():
        for h in range(hq):
            att[:, h * HD : (h + 1) * HD] = of[pl.ds(h, rows, stride=hq), :].astype(BF16)

    @pl.when(turn > 0)
    def _():
        for s, (owner, start, size, loff) in enumerate(segs):

            @pl.when(turn != owner)
            def _(s=s):
                ag_copy(s, 0).wait_recv()

        biases = jnp.concatenate([bias] * gq, axis=0)
        for j in range(kh):
            query = jnp.concatenate(
                [
                    qv[:, (j * gq + x) * HD : (j * gq + x + 1) * HD].astype(F32)
                    for x in range(gq)
                ],
                axis=0,
            )

            def mine_of(first):
                col = first + (kv_first(c) + j) * HD
                return jnp.concatenate([frall[col // fw, lax.rem(col, fw) // HD]] * gq, axis=0)

            score = lax.dot_general(
                query.astype(BF16),
                kv[:, j * HD : (j + 1) * HD],
                (((1,), (1,)), ((), ())),
                preferred_element_type=F32,
            )
            score = score * scale + biases
            mine = jnp.sum(query * mine_of(0), axis=1, keepdims=True) * scale
            top = jnp.maximum(jnp.max(score, axis=1, keepdims=True), mine)
            expo = jnp.exp(score - top)
            mine = jnp.exp(mine - top)
            denom = jnp.sum(expo, axis=1, keepdims=True) + mine
            weight = (expo / denom).astype(BF16)
            mine = (mine / denom).astype(BF16).astype(F32)
            result = jnp.dot(
                weight, kv[:, kw + j * HD : kw + (j + 1) * HD], preferred_element_type=F32
            )
            result = result + mine * mine_of(half)
            for x in range(gq):
                h = j * gq + x
                cached = of[pl.ds(h, rows, stride=hq), :]
                att[:, h * HD : (h + 1) * HD] = jnp.where(
                    landed, result[x * rows : (x + 1) * rows], cached
                ).astype(BF16)


    def drain(o, carry):
        d = peer(o)
        q_copy(d, c).wait_send()
        f_copy(d, c).wait_send()
        s_copy(d, c).wait_send()
        o_copy(d, c).wait_send()
        return carry

    lax.fori_loop(1, n, drain, 0)

    for s, (owner, start, size, loff) in enumerate(segs):

        @pl.when(turn == owner)
        def _(s=s, owner=owner):
            def drain_rs(o, carry):
                rs_copy(s, peer(o), c).wait_send()
                return carry

            lax.fori_loop(1, n, drain_rs, 0)
            for t in range(1, TURNS):
                if t != owner:
                    ag_copy(s, t).wait_send()

    @pl.when(turn == 0)
    def _():
        for s, seg in enumerate(segs):
            if seg[0] > 0:
                spread(s).wait_send()


def solution(mesh):
    n = mesh.shape["tp"]
    groups = mesh.shape["group"]

    def per_device(
        hidden, w_kv, plen, ostep, cache, clen, queries, fresh, logits, states, masks
    ):
        block, dl = hidden.shape
        rows, vdev = logits.shape
        own, npos, kvw = cache.shape
        hq = HEADS // n
        kw2 = 2 * max(1, hq // GQ) * HD
        oh = own * hq
        fw = fresh.shape[1]
        segs = segments(block)
        ns = len(segs)
        tmax = max(size + loff for _, _, size, loff in segs)
        dma = pltpu.SemaphoreType.DMA
        vmem = pl.BlockSpec(memory_space=pltpu.VMEM)
        anys = pl.BlockSpec(memory_space=pl.ANY)
        made = pl.pallas_call(
            functools.partial(kernel, n, groups),
            out_shape=(
                pltpu.VMEM(queries.shape, BF16),
                pltpu.VMEM(logits.shape, F32),
            ),
            in_specs=[anys] * 11,
            out_specs=(vmem, vmem),
            scratch_shapes=[pltpu.SMEM(x.shape, jnp.int32) for x in (plen, ostep, clen, states)]
            + [
                pltpu.VMEM((tmax, dl), BF16),
                pltpu.VMEM((n, dl, kw2), BF16),
                pltpu.VMEM((n, tmax, kw2), BF16),
                pltpu.VMEM((n, tmax, kw2), BF16),
                pltpu.VMEM((block, kw2), BF16),
                pltpu.VMEM(cache.shape, BF16),
                pltpu.VMEM(queries.shape, BF16),
                pltpu.VMEM((n, rows, fw), BF16),
                pltpu.VMEM(logits.shape, BF16),
                pltpu.VMEM((masks.shape[1] // HD,) + (masks.shape[0], HD), jnp.int32),
                pltpu.VMEM((masks.shape[1] // HD, rows, HD), jnp.int32),
                pltpu.VMEM((rows * hq, HD), F32),
                pltpu.VMEM((n, oh, HD), BF16),
                pltpu.VMEM((n, oh, HD), BF16),
                pltpu.VMEM((n, oh, HD), BF16),
                pltpu.VMEM((n, oh, HD), BF16),
                pltpu.VMEM((rows * hq, HD), F32),
                pltpu.VMEM((n, fw // HD, rows, HD), F32),
                pltpu.VMEM((n, rows, HD), F32),
                dma((6 + masks.shape[1] // HD,)),
                dma((n, 2)),
                dma((ns,)),
                dma((ns,)),
                dma((ns, n)),
                dma((ns, n)),
                dma((ns, TURNS)),
                dma((ns,)),
                dma((4,)),
                dma((n,)),
                dma((n,)),
                dma((n,)),
                dma((n,)),
                dma((n,)),
                dma((n,)),
                dma((n,)),
                dma((n,)),
            ],
            compiler_params=pltpu.CompilerParams(
                collective_id=0, has_side_effects=True, vmem_limit_bytes=60 * 1024 * 1024
            ),
        )(plen, ostep, clen, states, hidden, w_kv, cache, queries, fresh, logits, masks)
        return tuple(made)

    in_specs = (
        P("group", "tp"),
        P("tp", None),
        P(),
        P(),
        P(("group", "tp"), None, None),
        P(("group", "tp")),
        P("group", "tp"),
        P("group", "tp"),
        P("group", "tp"),
        P("group"),
        P(None, "tp"),
    )
    out_specs = (P("group", "tp"), P("group", "tp"))
    return jax.shard_map(
        per_device, mesh=mesh, in_specs=in_specs, out_specs=out_specs, check_vma=False
    )
```
